512 devices in a mesh: leaf: 8 (over y), blk: 64 (over x, z, core).
Axes of the slice: x: 4, y: 8, z: 8, core: 2. Of those that a mesh axis runs over, the one named last changes fastest.
Arguments:
- right_sides: bfloat16 [8, 64, 4, 512, 32], P('leaf', 'blk'), may hold values from -6 to 6
- inverses: bfloat16 [8, 64, 4, 512, 512], P('leaf', 'blk')
- couplings: bfloat16 [8, 64, 3, 256, 512], P('leaf', 'blk'), may hold values from -0.25 to 0.25
- widths: int32 [8, 64, 4], P('leaf', 'blk'), may hold values from 1 to 4, as said below
- targets: int32 [3, 8, 64, 64], replicated, may hold values from 0 to 16383, as said below
Outputs:
- solution: bfloat16 [8, 64, 4, 512, 32], P('leaf', 'blk')
The draws below stay inside these ranges and needn't reach their ends.
Inputs may be any that keep to these rules, and one draw needn't show every extreme that they name: `widths`: at every level some device has 4 live block units. `targets`: every piece names live rows of its target supernode. At level l, with partner group g XOR 2 ** (l % log2(8)), devices (g, j) and (partner, j) together send at most 3 pieces to owners of blk index d, counting both groups. For each such pair of groups there are one blk index h and one of the two groups such that every pair (g, j), (partner, j) sends exactly 3 pieces to index h of that group, all from one of its two devices.
All inputs are finite; a program needn't handle non-finite values.
Results may differ from the reference program's by a relative error of at most 0.012.
Values may be sent and summed in bfloat16 or wider, within the bound.
A program may use at most 64 MiB of HBM per device.

```python
import math
import jax
import jax.numpy as jnp
import numpy as np

R = 32
BLOCK = 128
SNB = 4
LEVELS = 4
PIECE = 4
PIECES = 64
W = 512
PR = 256
POS = 128
CAP = 3
N_LEAF = 8
N_BLK = 64


def live_table(key):
    base = jax.random.fold_in(key, 11)
    first, second = jax.random.split(base)
    counts = jax.random.randint(first, (N_LEAF, N_BLK, LEVELS), 1, SNB + 1)
    chosen = jax.random.randint(second, (LEVELS,), 0, N_LEAF * N_BLK)
    flat_ids = jnp.arange(N_LEAF * N_BLK).reshape(N_LEAF, N_BLK)
    counts = jnp.where(flat_ids[:, :, None] == chosen[None, None, :], SNB, counts)
    return counts.astype(jnp.int32)


def draw_widths(key, part):
    return live_table(key)


def draw_targets(key, part):
    counts = live_table(key)
    base = jax.random.fold_in(key, 23)
    leaf_bits = N_LEAF.bit_length() - 1
    group_ids = np.arange(N_LEAF, dtype=np.int32)
    pair_slots = (N_BLK - 1) * CAP
    spare = 2 * PIECES - CAP
    layers = []
    for level in range(LEVELS - 1):
        keys = jax.random.split(jax.random.fold_in(base, level), 7)
        shift_bit = level % leaf_bits
        low_ids = group_ids & ~(1 << shift_bit)
        mine_bits = group_ids >> shift_bit & 1
        hot_blk = jax.random.randint(keys[0], (N_LEAF,), 0, N_BLK)[low_ids]
        hot_pick = jax.random.randint(keys[1], (N_LEAF,), 0, 2)[low_ids]
        hot_group = jnp.asarray(low_ids) + hot_pick * (1 << shift_bit)
        heavy = jax.random.randint(keys[2], (N_LEAF, N_BLK), 0, 2)[low_ids]
        perm_keys = jax.random.split(keys[3], N_LEAF * N_BLK)
        perms = jax.vmap(lambda one: jax.random.permutation(one, pair_slots))(perm_keys)
        perms = perms.reshape(N_LEAF, N_BLK, pair_slots)[low_ids][:, :, :spare]
        dest_rest = perms // CAP
        dest_rest = dest_rest + (dest_rest >= hot_blk[:, None, None]).astype(jnp.int32)
        side_rest = jax.random.randint(keys[4], (N_LEAF, N_BLK, spare), 0, 2)[low_ids]
        hot_side = (hot_group != jnp.asarray(group_ids)).astype(jnp.int32)
        hot_dest = jnp.broadcast_to(hot_blk[:, None, None], (N_LEAF, N_BLK, CAP))
        hot_sides = jnp.broadcast_to(hot_side[:, None, None], (N_LEAF, N_BLK, CAP))
        dest_heavy = jnp.concatenate([hot_dest, dest_rest[:, :, :PIECES - CAP]], axis=2)
        side_heavy = jnp.concatenate([hot_sides, side_rest[:, :, :PIECES - CAP]], axis=2)
        dest_light = dest_rest[:, :, PIECES - CAP:]
        side_light = side_rest[:, :, PIECES - CAP:]
        is_heavy = (heavy == jnp.asarray(mine_bits)[:, None])[:, :, None]
        dest_blk = jnp.where(is_heavy, dest_heavy, dest_light)
        side_bit = jnp.where(is_heavy, side_heavy, side_light)
        target_group = jnp.bitwise_xor(jnp.asarray(group_ids)[:, None, None], side_bit * (1 << shift_bit))
        live_rows = counts[target_group, dest_blk, level + 1] * (BLOCK // PIECE)
        row_place = jax.random.randint(keys[5], (N_LEAF, N_BLK, PIECES), 0, live_rows)
        codes = (side_bit * N_BLK + dest_blk) * POS + row_place
        order_keys = jax.random.split(keys[6], N_LEAF * N_BLK)
        orders = jax.vmap(lambda one: jax.random.permutation(one, PIECES))(order_keys).reshape(N_LEAF, N_BLK, PIECES)
        layers.append(jnp.take_along_axis(codes, orders, axis=2))
    return jnp.stack(layers, axis=0).astype(jnp.int32)


def draw_inverses(key, part):
    shape = (N_LEAF, N_BLK, LEVELS, W, W)
    first, second = jax.random.split(key)
    row_ids = jnp.arange(W)
    below = row_ids[:, None] > row_ids[None, :]
    on_diag = row_ids[:, None] == row_ids[None, :]
    lower = jax.random.normal(first, shape, jnp.float32) * (0.35 / math.sqrt(W))
    diagonal = jnp.exp(jax.random.uniform(second, shape[:-1], jnp.float32, math.log(0.6), math.log(1.6)))
    full = jnp.where(below, lower, 0.0) + jnp.where(on_diag, diagonal[..., None], 0.0)
    return full.astype(jnp.bfloat16)


def block_scale(key, shape, shards, least, high):
    loudness, own = 1.0, jax.random.fold_in(key, 6)
    for axis_at, blocks in shards:
        steps = jnp.exp(jax.random.uniform(jax.random.fold_in(own, axis_at), (blocks,), jnp.float32, least / len(shards), high / len(shards)))
        loudness = loudness * jnp.repeat(steps, shape[axis_at] // blocks).reshape([-1 if axis == axis_at else 1 for axis in range(len(shape))])
    return loudness


def centred(key, extent, scale, bound, shards=(), held_as=jnp.bfloat16):
    values = scale * jax.random.normal(key, extent, jnp.float32)
    if shards:
        values = values * block_scale(key, extent, shards, -0.22, 0.18)
    return jnp.clip(values, -bound, bound).astype(held_as)


def setup_inputs(seed: int = 0) -> dict:
    seeds = jax.random.split(jax.random.key(seed), 6)
    right_sides = centred(seeds[0], (N_LEAF, N_BLK, LEVELS, W, R), 1.0, 6.0, ((0, 8), (1, 64)))
    inverses = draw_inverses(jax.random.fold_in(seeds[5], 71), 0)
    couplings = centred(seeds[2], (N_LEAF, N_BLK, LEVELS - 1, PR, W), W ** -0.5, 0.25, ((0, 8), (1, 64)))
    widths = draw_widths(jax.random.fold_in(seeds[5], 71), 0)
    targets = draw_targets(jax.random.fold_in(seeds[5], 71), 0)
    return {"right_sides": right_sides, "inverses": inverses, "couplings": couplings, "widths": widths, "targets": targets}


def decode_codes(code_list):
    side_bit = code_list // (N_BLK * POS)
    dest_blk = (code_list // POS) % N_BLK
    row_place = code_list % POS
    return side_bit, dest_blk, row_place


def reference(right_sides, inverses, couplings, widths, targets):
    leaf_bits = N_LEAF.bit_length() - 1
    row_index = jnp.arange(W, dtype=jnp.int32)
    group_index = jnp.arange(N_LEAF, dtype=jnp.int32)[:, None, None]
    row_masks = []
    for level in range(LEVELS):
        live_rows = widths[:, :, level, None] * BLOCK
        row_masks.append((row_index[None, None, :] < live_rows).astype(jnp.float32)[..., None])
    forward = []
    flat_targets = []
    incoming = None
    for level in range(LEVELS):
        if level == 0:
            residual = right_sides[:, :, 0]
        else:
            residual = (right_sides[:, :, level].astype(jnp.float32) - incoming).astype(jnp.bfloat16)
        product = jnp.einsum("gjab,gjbr->gjar", inverses[:, :, level].astype(jnp.float32), residual.astype(jnp.float32))
        solved = (row_masks[level] * product).astype(jnp.bfloat16)
        forward.append(solved)
        if level + 1 < LEVELS:
            pieces = jnp.einsum("gjab,gjbr->gjar", couplings[:, :, level].astype(jnp.float32), solved.astype(jnp.float32))
            pieces = pieces.astype(jnp.bfloat16).reshape(N_LEAF * N_BLK * PIECES, PIECE * R)
            side_bit, dest_blk, row_place = decode_codes(targets[level])
            target_group = jnp.bitwise_xor(group_index, side_bit * (2 ** (level % leaf_bits)))
            flat_index = ((target_group * N_BLK + dest_blk) * POS + row_place).reshape(-1).astype(jnp.int32)
            flat_targets.append(flat_index)
            summed = jnp.zeros((N_LEAF * N_BLK * POS, PIECE * R), jnp.float32).at[flat_index].add(pieces.astype(jnp.float32))
            incoming = summed.reshape(N_LEAF, N_BLK, W, R)
    solution = [None] * LEVELS
    for level in reversed(range(LEVELS)):
        if level + 1 == LEVELS:
            back_side = forward[level]
        else:
            above_rows = solution[level + 1].reshape(N_LEAF * N_BLK * POS, PIECE * R)
            gathered = above_rows[flat_targets[level]].reshape(N_LEAF, N_BLK, PR, R)
            update = jnp.einsum("gjba,gjbr->gjar", couplings[:, :, level].astype(jnp.float32), gathered.astype(jnp.float32))
            back_side = (forward[level].astype(jnp.float32) - update).astype(jnp.bfloat16)
        masked = row_masks[level] * back_side.astype(jnp.float32)
        product = jnp.einsum("gjba,gjbr->gjar", inverses[:, :, level].astype(jnp.float32), masked)
        solution[level] = (row_masks[level] * product).astype(jnp.bfloat16)
    return jnp.stack(solution, axis=2)
```

```python
import functools

import jax
import jax.numpy as jnp
from jax import lax
from jax.experimental import pallas as pl
from jax.experimental.pallas import tpu as pltpu
from jax.sharding import PartitionSpec as P

BLOCK = 128
SLOTS = 4
MESH = pl.DeviceIdType.MESH
NN = (((1,), (0,)), ((), ()))
NT = (((1,), (1,)), ((), ()))
TN = (((0,), (0,)), ((), ()))


def dot(left, right, dims=NN):
    return lax.dot_general(left, right, dims, preferred_element_type=jnp.float32)


def iota(shape, axis):
    return lax.broadcasted_iota(jnp.int32, shape, axis)


def one_hot(condition):
    return condition.astype(jnp.float32).astype(jnp.bfloat16)


def peer_of(step, me, sizes):
    xs, zs, cores = sizes
    z_at, x_at, core_at = step // (xs * cores), step // cores % xs, step % cores
    z_off = zs // 2 + (z_at + 1) // 2 * (1 - 2 * (z_at % 2))
    x_off = xs // 2 + (x_at + 1) // 2 * (1 - 2 * (x_at % 2))
    x = (me // (zs * cores) + x_off) % xs
    z = (me // cores % zs + z_off) % zs
    core = (me % cores + cores - 1 - core_at) % cores
    return (x * zs + z) * cores + core


def kernel(
    sizes,
    b_hbm,
    inv_hbm,
    cpl_hbm,
    wid_ref,
    tgt_hbm,
    out_ref,
    b_ref,
    inv_ref,
    cpl_ref,
    tbl_ref,
    send_mat,
    back_mat,
    take_mat,
    piece_out,
    piece_in,
    slot_out,
    slot_in,
    load_sem,
    pair_send,
    pair_recv,
    slot_send,
    slot_recv,
):
    levels, cols, width = b_ref.shape
    rows = cpl_ref.shape[1]
    owners, pieces = tbl_ref.shape[2], tbl_ref.shape[3]
    lanes = rows // pieces * cols
    piece_rows = rows // pieces
    places = width // piece_rows
    leaf_bits = lax.axis_size("leaf").bit_length() - 1
    group, me = lax.axis_index("leaf"), lax.axis_index("blk")
    slot_rows = owners * SLOTS

    def partner_of(level):
        bit = 1 << level % leaf_bits
        return group + bit - 2 * bit * (group // bit % 2)

    loads = [pltpu.make_async_copy(b_hbm, b_ref, load_sem.at[0])]
    for level in range(levels - 1):
        for side, source in enumerate((group, partner_of(level))):
            loads.append(
                pltpu.make_async_copy(
                    tgt_hbm.at[level, source],
                    tbl_ref.at[level, side],
                    load_sem.at[1 + 2 * level + side],
                )
            )
    base = 2 * levels - 1
    inv_loads = [
        pltpu.make_async_copy(inv_hbm.at[n], inv_ref.at[n], load_sem.at[base + n])
        for n in range(levels)
    ]
    cpl_loads = [
        pltpu.make_async_copy(cpl_hbm.at[n], cpl_ref.at[n], load_sem.at[base + levels + n])
        for n in range(levels - 1)
    ]
    loads[0].start()
    inv_loads[0].start()
    cpl_loads[0].start()
    for copy in loads[1:]:
        copy.start()
    for copy in inv_loads[1:] + cpl_loads[1:]:
        copy.start()

    barrier = pltpu.get_barrier_semaphore()

    def greet(step, carry):
        pl.semaphore_signal(
            barrier, inc=1, device_id=(group, peer_of(step, me, sizes)), device_id_type=MESH
        )
        return carry

    lax.fori_loop(0, owners - 1, greet, 0)
    for level in range(levels - 1):
        pl.semaphore_signal(barrier, inc=1, device_id=(partner_of(level), me), device_id_type=MESH)

    before = one_hot(iota((2 * pieces, 2 * pieces), 0) < iota((2 * pieces, 2 * pieces), 1))
    gather_rows = one_hot(iota((pieces, rows), 1) // piece_rows == iota((pieces, rows), 0))
    repeat = one_hot(iota((slot_rows, owners), 0) // SLOTS == iota((slot_rows, owners), 1))
    slot_rank = (iota((slot_rows, 2 * pieces), 0) % SLOTS).astype(jnp.float32)
    on_pair = iota((1, 2 * pieces), 1) // pieces

    def row_mask(level):
        return (iota((1, width), 1) < wid_ref[0, level] * BLOCK).astype(jnp.float32)

    def codes(own, pair):
        code = jnp.concatenate([own, pair], axis=1)
        ok = code // (owners * places) == on_pair
        return ok, code // places % owners, code % places

    def make_send(level):
        mine = tbl_ref[level, 0, pl.ds(me, 1), :]
        pair = tbl_ref[level, 1, pl.ds(me, 1), :]
        ok, dest, _ = codes(mine, pair)
        dest = jnp.where(ok, dest, -1)
        hit = (iota((slot_rows, 2 * pieces), 0) // SLOTS == dest).astype(jnp.float32)
        count = dot(hit.astype(jnp.bfloat16), before)
        chosen = jnp.where(count == slot_rank, hit, 0.0).astype(jnp.bfloat16)
        send_mat[level] = chosen

    def make_back(level):
        back_mat[level] = jnp.transpose(send_mat[level].astype(jnp.float32)).astype(jnp.bfloat16)

    def make_take(level):
        ok, dest, place = codes(tbl_ref[level, 0], tbl_ref[level, 1])
        match = (ok & (dest == me)).astype(jnp.float32)
        spot = dot(repeat, (match * (place + 1).astype(jnp.float32)).astype(jnp.bfloat16))
        hit = dot(repeat, match.astype(jnp.bfloat16))
        count = dot(hit.astype(jnp.bfloat16), before)
        spot = jnp.sum(jnp.where(count == slot_rank, spot, 0.0), axis=1, keepdims=True)
        at = (iota((1, width), 1) // piece_rows + 1).astype(jnp.float32)
        take_mat[level] = one_hot(spot == at)

    def spread(value):
        turn = iota(value.shape, 1) % piece_rows
        return jnp.concatenate(
            [jnp.where(turn == i, value, 0.0) for i in range(piece_rows)], axis=0
        ).astype(jnp.bfloat16)

    def collect(value):
        turn = iota((cols, value.shape[1]), 1) % piece_rows
        out = value[:cols]
        for i in range(1, piece_rows):
            out = jnp.where(turn == i, value[i * cols : (i + 1) * cols], out)
        return out

    def pair_copy(phase, level):
        return pltpu.make_async_remote_copy(
            src_ref=piece_out.at[phase],
            dst_ref=piece_in.at[phase],
            send_sem=pair_send.at[phase],
            recv_sem=pair_recv.at[phase],
            device_id=(partner_of(level), me),
            device_id_type=MESH,
        )

    def send_slots(phase, value):
        slot_out[phase] = value.reshape(owners, SLOTS, lanes)

        def send(step, carry):
            peer = peer_of(step, me, sizes)
            pltpu.make_async_remote_copy(
                src_ref=slot_out.at[phase, peer],
                dst_ref=slot_in.at[phase, me],
                send_sem=slot_send.at[phase],
                recv_sem=slot_recv.at[phase],
                device_id=(group, peer),
                device_id_type=MESH,
            ).start()
            return carry

        lax.fori_loop(0, owners - 1, send, 0)
        pltpu.make_async_copy(
            slot_out.at[phase, me], slot_in.at[phase, me], slot_recv.at[phase]
        ).start()

    def slots_arrived(phase):
        pltpu.make_async_copy(slot_out.at[phase], slot_in.at[phase], slot_recv.at[phase]).wait()
        return slot_in[phase].reshape(slot_rows, lanes)

    forward = []
    for level in range(levels):
        if level == 0:
            loads[0].wait()
            residual = b_ref[0]
            inv_loads[0].wait()
        solved = row_mask(level) * dot(residual, inv_ref[level], NT)
        solved = solved.astype(jnp.bfloat16)
        forward.append(solved)
        if level + 1 == levels:
            break
        if level == 0:
            cpl_loads[0].wait()
        blocks = dot(solved, cpl_ref[level], NT)
        own = dot(gather_rows, spread(blocks), NT).astype(jnp.bfloat16)
        piece_out[level] = own
        if level == 0:
            pl.semaphore_wait(barrier, owners - 1 + levels - 1)
        copy = pair_copy(level, level)
        copy.start()
        if level == 0:
            for load in loads[1:]:
                load.wait()
            make_send(0)
        copy.wait_recv()
        both = jnp.concatenate([own, piece_in[level]], axis=0)
        send_slots(level, dot(send_mat[level], both).astype(jnp.bfloat16))
        make_take(level)
        if level == 0:
            for load in inv_loads[1:] + cpl_loads[1:]:
                load.wait()
        if level + 2 < levels:
            make_send(level + 1)
        make_back(level)
        arrived = slots_arrived(level)
        incoming = collect(dot(arrived, take_mat[level], TN))
        residual = (b_ref[level + 1].astype(jnp.float32) - incoming).astype(jnp.bfloat16)

    above = None
    for level in reversed(range(levels)):
        if level + 1 == levels:
            back_side = forward[level].astype(jnp.float32)
        else:
            phase = levels - 1 + level
            reply = dot(take_mat[level], spread(above), NT).astype(jnp.bfloat16)
            send_slots(phase, reply)
            arrived = slots_arrived(phase)
            both = dot(back_mat[level], arrived)
            piece_out[phase] = both[pieces:].astype(jnp.bfloat16)
            copy = pair_copy(phase, level)
            copy.start()
            copy.wait_recv()
            gathered = (both[:pieces] + piece_in[phase].astype(jnp.float32)).astype(jnp.bfloat16)
            rows_in = collect(dot(gathered, gather_rows, TN)).astype(jnp.bfloat16)
            back_side = forward[level].astype(jnp.float32) - dot(rows_in, cpl_ref[level])
            back_side = back_side.astype(jnp.bfloat16).astype(jnp.float32)
        masked = (row_mask(level) * back_side).astype(jnp.bfloat16)
        answer = (row_mask(level) * dot(masked, inv_ref[level])).astype(jnp.bfloat16)
        out_ref[level] = answer
        above = answer.astype(jnp.float32)

    for phase in range(2 * (levels - 1)):
        pair_copy(phase, phase % (levels - 1)).wait_send()
        pltpu.make_async_copy(
            slot_out.at[phase, pl.ds(0, owners - 1)],
            slot_in.at[phase, pl.ds(0, owners - 1)],
            slot_send.at[phase],
        ).wait()


def shards(right_sides, inverses, couplings, widths, targets):
    owners = lax.axis_size("blk")
    right = jnp.swapaxes(right_sides[0, 0], 1, 2)
    inverse, coupling = inverses[0, 0], couplings[0, 0]
    levels, cols, width = right.shape
    rows, pieces = coupling.shape[1], targets.shape[3]
    lanes = rows // pieces * cols
    phases = 2 * (levels - 1)
    slot_rows = owners * SLOTS
    hbm = pl.BlockSpec(memory_space=pl.ANY)
    out = pl.pallas_call(
        functools.partial(kernel, (4, 8, 2)),
        out_shape=jax.ShapeDtypeStruct((levels, cols, width), jnp.bfloat16),
        in_specs=[hbm, hbm, hbm, pl.BlockSpec(memory_space=pltpu.SMEM), hbm],
        out_specs=pl.BlockSpec(memory_space=pltpu.VMEM),
        scratch_shapes=[
            pltpu.VMEM((levels, cols, width), jnp.bfloat16),
            pltpu.VMEM((levels, width, width), jnp.bfloat16),
            pltpu.VMEM((levels - 1, rows, width), jnp.bfloat16),
            pltpu.VMEM((levels - 1, 2, owners, pieces), jnp.int32),
            pltpu.VMEM((levels - 1, slot_rows, 2 * pieces), jnp.bfloat16),
            pltpu.VMEM((levels - 1, 2 * pieces, slot_rows), jnp.bfloat16),
            pltpu.VMEM((levels - 1, slot_rows, width), jnp.bfloat16),
            pltpu.VMEM((phases, pieces, lanes), jnp.bfloat16),
            pltpu.VMEM((phases, pieces, lanes), jnp.bfloat16),
            pltpu.VMEM((phases, owners, SLOTS, lanes), jnp.bfloat16),
            pltpu.VMEM((phases, owners, SLOTS, lanes), jnp.bfloat16),
            pltpu.SemaphoreType.DMA((4 * levels - 2,)),
            pltpu.SemaphoreType.DMA((phases,)),
            pltpu.SemaphoreType.DMA((phases,)),
            pltpu.SemaphoreType.DMA((phases,)),
            pltpu.SemaphoreType.DMA((phases,)),
        ],
        compiler_params=pltpu.CompilerParams(collective_id=0, has_side_effects=True),
    )(right, inverse, coupling, widths[0], targets)
    return jnp.swapaxes(out, 1, 2)[None, None]


def solution(mesh):
    return jax.shard_map(
        shards,
        mesh=mesh,
        in_specs=(
            P("leaf", "blk", None, None, None),
            P("leaf", "blk", None, None, None),
            P("leaf", "blk", None, None, None),
            P("leaf", "blk", None),
            P(),
        ),
        out_specs=P("leaf", "blk", None, None, None),
        check_vma=False,
    )
```

```python
import functools

import jax
import jax.numpy as jnp
from jax import lax
from jax.experimental import pallas as pl
from jax.experimental.pallas import tpu as pltpu
from jax.sharding import PartitionSpec as P

BLOCK = 128
SLOTS = 4
MESH = pl.DeviceIdType.MESH
NN = (((1,), (0,)), ((), ()))
NT = (((1,), (1,)), ((), ()))
TN = (((0,), (0,)), ((), ()))


def dot(left, right, dims=NN):
    return lax.dot_general(left, right, dims, preferred_element_type=jnp.float32)


def iota(shape, axis):
    return lax.broadcasted_iota(jnp.int32, shape, axis)


def one_hot(condition):
    return condition.astype(jnp.float32).astype(jnp.bfloat16)


def each_owner(me, sizes, visit):
    xs, zs, cores = sizes
    z, core = lax.rem(lax.div(me, cores), zs), lax.rem(me, cores)
    x = lax.div(me, zs * cores)
    x_order = sorted(range(xs), key=lambda off: -min(off, xs - off))
    columns = [
        lax.rem(x + off, xs) * (zs * cores) + lax.rem(core + 1 + n, cores)
        for off in x_order
        for n in range(cores)
    ]

    def plane(step, carry):
        off = zs // 2 + lax.div(step + 1, 2) * (1 - 2 * lax.rem(step, 2))
        row = lax.rem(z + off, zs) * cores
        for column in columns:
            visit(column + row, False)
        return carry

    lax.fori_loop(0, zs - 1, plane, 0)
    for column in columns[:-1]:
        visit(column + z * cores, False)
    visit(me, True)


def kernel(
    sizes,
    b_hbm,
    inv_hbm,
    cpl_hbm,
    wid_ref,
    tgt_hbm,
    out_ref,
    b_ref,
    inv_ref,
    cpl_ref,
    tbl_ref,
    send_mat,
    take_mat,
    slot_out,
    slot_in,
    load_sem,
    slot_send,
    slot_recv,
    near_sem,
):
    levels, cols, width = b_ref.shape
    rows = cpl_ref.shape[1]
    owners, pieces = tbl_ref.shape[2], tbl_ref.shape[3]
    lanes = rows // pieces * cols
    piece_rows = rows // pieces
    places = width // piece_rows
    leaf_bits = lax.axis_size("leaf").bit_length() - 1
    group, me = lax.axis_index("leaf"), lax.axis_index("blk")
    slot_rows = 2 * owners * SLOTS

    def partner_of(level):
        bit = 1 << level % leaf_bits
        return group + bit - 2 * bit * (group // bit % 2)

    loads = [pltpu.make_async_copy(b_hbm, b_ref, load_sem.at[0])]
    for level in range(levels - 1):
        for side, source in enumerate((group, partner_of(level))):
            loads.append(
                pltpu.make_async_copy(
                    tgt_hbm.at[level, source],
                    tbl_ref.at[level, side],
                    load_sem.at[1 + 2 * level + side],
                )
            )
    base = 2 * levels - 1
    inv_loads = [
        pltpu.make_async_copy(inv_hbm.at[n], inv_ref.at[n], load_sem.at[base + n])
        for n in range(levels)
    ]
    cpl_loads = [
        pltpu.make_async_copy(cpl_hbm.at[n], cpl_ref.at[n], load_sem.at[base + levels + n])
        for n in range(levels - 1)
    ]
    loads[1].start()
    loads[0].start()
    inv_loads[0].start()
    cpl_loads[0].start()
    for copy in loads[2:] + inv_loads[1:] + cpl_loads[1:]:
        copy.start()

    barrier = pltpu.get_barrier_semaphore()

    def signal(semaphore, leaf, blk):
        pl.semaphore_signal(semaphore, inc=1, device_id=(leaf, blk), device_id_type=MESH)

    def greet(owner, last):
        if not last:
            signal(barrier, group, owner)

    each_owner(me, sizes, greet)
    for level in range(levels - 1):
        signal(barrier, partner_of(level), me)

    before = one_hot(iota((pieces, pieces), 0) < iota((pieces, pieces), 1))
    widen = one_hot(iota((pieces, rows), 1) // piece_rows == iota((pieces, rows), 0))
    repeat = one_hot(iota((slot_rows, 2 * owners), 0) // SLOTS == iota((slot_rows, 2 * owners), 1))
    slot_rank = (iota((slot_rows, pieces), 0) % SLOTS).astype(jnp.float32)

    def row_mask(level):
        return (iota((1, width), 1) < wid_ref[0, level] * BLOCK).astype(jnp.float32)

    def make_send(level):
        dest = tbl_ref[level, 0, pl.ds(me, 1), :] // places
        hit = (iota((slot_rows, pieces), 0) // SLOTS == dest).astype(jnp.float32)
        count = dot(hit.astype(jnp.bfloat16), before)
        chosen = jnp.where(count == slot_rank, hit, 0.0).astype(jnp.bfloat16)
        send_mat[level] = dot(chosen, widen).astype(jnp.bfloat16)

    def make_take(level):
        code = jnp.concatenate([tbl_ref[level, 0], tbl_ref[level, 1]], axis=0)
        wanted = iota((2 * owners, 1), 0) // owners * owners + me
        match = (code // places == wanted).astype(jnp.float32)
        spot = dot(repeat, (match * (code % places + 1).astype(jnp.float32)).astype(jnp.bfloat16))
        hit = dot(repeat, match.astype(jnp.bfloat16))
        count = dot(hit.astype(jnp.bfloat16), before)
        spot = jnp.sum(jnp.where(count == slot_rank, spot, 0.0), axis=1, keepdims=True)
        at = (iota((1, width), 1) // piece_rows + 1).astype(jnp.float32)
        take_mat[level] = one_hot(spot == at)

    def spread(value):
        turn = iota(value.shape, 1) % piece_rows
        return jnp.concatenate(
            [jnp.where(turn == i, value, 0.0) for i in range(piece_rows)], axis=0
        ).astype(jnp.bfloat16)

    def collect(value):
        turn = iota((cols, value.shape[1]), 1) % piece_rows
        out = value[:cols]
        for i in range(1, piece_rows):
            out = jnp.where(turn == i, value[i * cols : (i + 1) * cols], out)
        return out

    def send_slots(phase, level, value):
        slot_out[phase] = value.astype(jnp.bfloat16).reshape(2, owners, SLOTS, lanes)
        partner = partner_of(level)

        def send(owner, last):
            for side in (1, 0):
                if side == 0 and last:
                    pltpu.make_async_copy(
                        slot_out.at[phase, 0, me], slot_in.at[phase, 0, me], slot_recv.at[phase]
                    ).start()
                    continue
                pltpu.make_async_remote_copy(
                    src_ref=slot_out.at[phase, side, owner],
                    dst_ref=slot_in.at[phase, side, me],
                    send_sem=slot_send.at[phase],
                    recv_sem=slot_recv.at[phase],
                    device_id=(partner if side else group, owner),
                    device_id_type=MESH,
                ).start()

        each_owner(me, sizes, send)

    def slots_arrived(phase):
        pltpu.make_async_copy(slot_out.at[phase], slot_in.at[phase], slot_recv.at[phase]).wait()
        return slot_in[phase].reshape(slot_rows, lanes)

    forward = []
    for level in range(levels):
        if level == 0:
            loads[1].wait()
            make_send(0)
            loads[0].wait()
            residual = b_ref[0]
            inv_loads[0].wait()
        solved = row_mask(level) * dot(residual, inv_ref[level], NT)
        solved = solved.astype(jnp.bfloat16)
        forward.append(solved)
        if level + 1 == levels:
            break
        if level == 0:
            cpl_loads[0].wait()
        blocks = dot(solved, cpl_ref[level], NT)
        buffer = dot(send_mat[level], spread(blocks), NT)
        if level == 0:
            pl.semaphore_wait(barrier, owners - 1 + levels - 1)
            signal(near_sem, partner_of(0), me)
            pl.semaphore_wait(near_sem, 1)
        send_slots(level, level, buffer)
        if level == 0:
            for load in loads[2:] + inv_loads[1:] + cpl_loads[1:]:
                load.wait()
        make_take(level)
        if level + 2 < levels:
            make_send(level + 1)
        arrived = slots_arrived(level)
        incoming = collect(dot(arrived, take_mat[level], TN))
        residual = (b_ref[level + 1].astype(jnp.float32) - incoming).astype(jnp.bfloat16)

    above = None
    for level in reversed(range(levels)):
        if level + 1 == levels:
            back_side = forward[level].astype(jnp.float32)
        else:
            phase = levels - 1 + level
            send_slots(phase, level, dot(take_mat[level], spread(above), NT))
            arrived = slots_arrived(phase)
            rows_in = collect(dot(arrived, send_mat[level], TN)).astype(jnp.bfloat16)
            back_side = forward[level].astype(jnp.float32) - dot(rows_in, cpl_ref[level])
            back_side = back_side.astype(jnp.bfloat16).astype(jnp.float32)
        masked = (row_mask(level) * back_side).astype(jnp.bfloat16)
        answer = (row_mask(level) * dot(masked, inv_ref[level])).astype(jnp.bfloat16)
        out_ref[level] = answer
        above = answer.astype(jnp.float32)

    for phase in range(2 * (levels - 1)):
        for side, count in ((0, owners - 1), (1, owners)):
            pltpu.make_async_copy(
                slot_out.at[phase, side, pl.ds(0, count)],
                slot_in.at[phase, side, pl.ds(0, count)],
                slot_send.at[phase],
            ).wait()


def shards(right_sides, inverses, couplings, widths, targets):
    owners = lax.axis_size("blk")
    right = jnp.swapaxes(right_sides[0, 0], 1, 2)
    inverse, coupling = inverses[0, 0], couplings[0, 0]
    levels, cols, width = right.shape
    rows, pieces = coupling.shape[1], targets.shape[3]
    lanes = rows // pieces * cols
    phases = 2 * (levels - 1)
    slot_rows = 2 * owners * SLOTS
    hbm = pl.BlockSpec(memory_space=pl.ANY)
    out = pl.pallas_call(
        functools.partial(kernel, (4, 8, 2)),
        out_shape=jax.ShapeDtypeStruct((levels, cols, width), jnp.bfloat16),
        in_specs=[hbm, hbm, hbm, pl.BlockSpec(memory_space=pltpu.SMEM), hbm],
        out_specs=pl.BlockSpec(memory_space=pltpu.VMEM),
        scratch_shapes=[
            pltpu.VMEM((levels, cols, width), jnp.bfloat16),
            pltpu.VMEM((levels, width, width), jnp.bfloat16),
            pltpu.VMEM((levels - 1, rows, width), jnp.bfloat16),
            pltpu.VMEM((levels - 1, 2, owners, pieces), jnp.int32),
            pltpu.VMEM((levels - 1, slot_rows, rows), jnp.bfloat16),
            pltpu.VMEM((levels - 1, slot_rows, width), jnp.bfloat16),
            pltpu.VMEM((phases, 2, owners, SLOTS, lanes), jnp.bfloat16),
            pltpu.VMEM((phases, 2, owners, SLOTS, lanes), jnp.bfloat16),
            pltpu.SemaphoreType.DMA((4 * levels - 2,)),
            pltpu.SemaphoreType.DMA((phases,)),
            pltpu.SemaphoreType.DMA((phases,)),
            pltpu.SemaphoreType.REGULAR,
        ],
        compiler_params=pltpu.CompilerParams(collective_id=0, has_side_effects=True),
    )(right, inverse, coupling, widths[0], targets)
    return jnp.swapaxes(out, 1, 2)[None, None]


def solution(mesh):
    return jax.shard_map(
        shards,
        mesh=mesh,
        in_specs=(
            P("leaf", "blk", None, None, None),
            P("leaf", "blk", None, None, None),
            P("leaf", "blk", None, None, None),
            P("leaf", "blk", None),
            P(),
        ),
        out_specs=P("leaf", "blk", None, None, None),
        check_vma=False,
    )
```

```python
import functools

import jax
import jax.numpy as jnp
from jax import lax
from jax.experimental import pallas as pl
from jax.experimental.pallas import tpu as pltpu
from jax.sharding import PartitionSpec as P

BLOCK = 128
SLOTS = 4
MESH = pl.DeviceIdType.MESH
NN = (((1,), (0,)), ((), ()))
NT = (((1,), (1,)), ((), ()))
TN = (((0,), (0,)), ((), ()))


def dot(left, right, dims=NN):
    return lax.dot_general(left, right, dims, preferred_element_type=jnp.float32)


def iota(shape, axis):
    return lax.broadcasted_iota(jnp.int32, shape, axis)


def one_hot(condition):
    return condition.astype(jnp.float32).astype(jnp.bfloat16)


def each_owner(me, sizes, visit):
    xs, zs, cores = sizes
    z, core = lax.rem(lax.div(me, cores), zs), lax.rem(me, cores)
    x = lax.div(me, zs * cores)
    x_order = sorted(range(xs), key=lambda off: -min(off, xs - off))
    columns = [
        lax.rem(x + off, xs) * (zs * cores) + lax.rem(core + 1 + n, cores)
        for off in x_order
        for n in range(cores)
    ]

    def plane(step, carry):
        off = zs // 2 + lax.div(step + 1, 2) * (1 - 2 * lax.rem(step, 2))
        row = lax.rem(z + off, zs) * cores
        for column in columns:
            visit(column + row, False)
        return carry

    lax.fori_loop(0, zs - 1, plane, 0)
    for column in columns[:-1]:
        visit(column + z * cores, False)
    visit(me, True)


def kernel(
    sizes,
    b_hbm,
    inv_hbm,
    cpl_hbm,
    wid_hbm,
    tgt_hbm,
    out_ref,
    wid_ref,
    b_ref,
    inv_ref,
    cpl_ref,
    tbl_ref,
    send_mat,
    take_mat,
    fold_ref,
    base_ref,
    slot_out,
    slot_in,
    load_sem,
    slot_send,
    slot_recv,
    near_sem,
):
    levels, cols, width = b_ref.shape
    rows = cpl_ref.shape[1]
    owners, pieces = tbl_ref.shape[2], tbl_ref.shape[3]
    lanes = rows // pieces * cols
    piece_rows = rows // pieces
    places = width // piece_rows
    leaf_bits = lax.axis_size("leaf").bit_length() - 1
    group, me = lax.axis_index("leaf"), lax.axis_index("blk")
    slot_rows = 2 * owners * SLOTS

    def partner_of(level):
        bit = 1 << level % leaf_bits
        return group + bit - 2 * bit * (group // bit % 2)

    loads = [pltpu.make_async_copy(b_hbm, b_ref, load_sem.at[0])]
    for level in range(levels - 1):
        for side, source in enumerate((group, partner_of(level))):
            loads.append(
                pltpu.make_async_copy(
                    tgt_hbm.at[level, source],
                    tbl_ref.at[level, side],
                    load_sem.at[1 + 2 * level + side],
                )
            )
    base = 2 * levels - 1
    inv_loads = [
        pltpu.make_async_copy(inv_hbm.at[n], inv_ref.at[n], load_sem.at[base + n])
        for n in range(levels)
    ]
    cpl_loads = [
        pltpu.make_async_copy(cpl_hbm.at[n], cpl_ref.at[n], load_sem.at[base + levels + n])
        for n in range(levels - 1)
    ]
    wid_load = pltpu.make_async_copy(wid_hbm, wid_ref, load_sem.at[base + 2 * levels - 1])
    loads[1].start()
    loads[0].start()
    wid_load.start()
    inv_loads[0].start()
    cpl_loads[0].start()
    for copy in loads[2:] + inv_loads[1:] + cpl_loads[1:]:
        copy.start()

    barrier = pltpu.get_barrier_semaphore()

    def signal(semaphore, leaf, blk):
        pl.semaphore_signal(semaphore, inc=1, device_id=(leaf, blk), device_id_type=MESH)

    def greet(owner, last):
        if not last:
            signal(barrier, group, owner)

    for level in range(levels - 1):
        signal(barrier, partner_of(level), me)
    each_owner(me, sizes, greet)

    before = one_hot(iota((pieces, pieces), 0) < iota((pieces, pieces), 1))
    widen = one_hot(iota((pieces, rows), 1) // piece_rows == iota((pieces, rows), 0))
    repeat = one_hot(iota((slot_rows, 2 * owners), 0) // SLOTS == iota((slot_rows, 2 * owners), 1))
    slot_rank = (iota((slot_rows, pieces), 0) % SLOTS).astype(jnp.float32)

    def row_mask(level):
        return (iota((1, width), 1) < wid_ref[0, level] * BLOCK).astype(jnp.float32)

    def make_send(level):
        dest = tbl_ref[level, 0, pl.ds(me, 1), :] // places
        hit = (iota((slot_rows, pieces), 0) // SLOTS == dest).astype(jnp.float32)
        count = dot(hit.astype(jnp.bfloat16), before)
        chosen = jnp.where(count == slot_rank, hit, 0.0).astype(jnp.bfloat16)
        send_mat[level] = dot(chosen, widen).astype(jnp.bfloat16)

    def make_take(level):
        code = jnp.concatenate([tbl_ref[level, 0], tbl_ref[level, 1]], axis=0)
        wanted = iota((2 * owners, 1), 0) // owners * owners + me
        match = (code // places == wanted).astype(jnp.float32)
        spot = dot(repeat, (match * (code % places + 1).astype(jnp.float32)).astype(jnp.bfloat16))
        hit = dot(repeat, match.astype(jnp.bfloat16))
        count = dot(hit.astype(jnp.bfloat16), before)
        spot = jnp.sum(jnp.where(count == slot_rank, spot, 0.0), axis=1, keepdims=True)
        at = (iota((1, width), 1) // piece_rows + 1).astype(jnp.float32)
        take_mat[level] = one_hot(spot == at)

    def spread(value):
        turn = iota(value.shape, 1) % piece_rows
        return jnp.concatenate(
            [jnp.where(turn == i, value, 0.0) for i in range(piece_rows)], axis=0
        ).astype(jnp.bfloat16)

    def collect(value):
        turn = iota((cols, value.shape[1]), 1) % piece_rows
        out = value[:cols]
        for i in range(1, piece_rows):
            out = jnp.where(turn == i, value[i * cols : (i + 1) * cols], out)
        return out

    def send_slots(phase, level, value):
        slot_out[phase] = value.astype(jnp.bfloat16).reshape(2, owners, SLOTS, lanes)
        partner = partner_of(level)

        def send(owner, last):
            for side in (1, 0):
                if side == 0 and last:
                    pltpu.make_async_copy(
                        slot_out.at[phase, 0, me], slot_in.at[phase, 0, me], slot_recv.at[phase]
                    ).start()
                    continue
                pltpu.make_async_remote_copy(
                    src_ref=slot_out.at[phase, side, owner],
                    dst_ref=slot_in.at[phase, side, me],
                    send_sem=slot_send.at[phase],
                    recv_sem=slot_recv.at[phase],
                    device_id=(partner if side else group, owner),
                    device_id_type=MESH,
                ).start()

        each_owner(me, sizes, send)

    def slots_arrived(phase):
        pltpu.make_async_copy(slot_out.at[phase], slot_in.at[phase], slot_recv.at[phase]).wait()
        return slot_in[phase].reshape(slot_rows, lanes)

    def fold(level):
        live = (cpl_ref[level].astype(jnp.float32) * row_mask(level)).astype(jnp.bfloat16)
        fold_ref[level] = dot(live, inv_ref[level]).astype(jnp.bfloat16)

    def forward_of(level, residual):
        return (row_mask(level) * dot(residual, inv_ref[level], NT)).astype(jnp.bfloat16)

    def settled(level, forward):
        return dot(forward, inv_ref[level])

    top = levels - 1
    loads[1].wait()
    make_send(0)
    loads[0].wait()
    inv_loads[0].wait()
    wid_load.wait()
    solved = forward_of(0, b_ref[0])
    cpl_loads[0].wait()
    blocks = dot(solved, cpl_ref[0], NT)
    base_ref[0] = settled(0, solved)
    for level in range(top):
        buffer = dot(send_mat[level], spread(blocks), NT)
        if level == 0:
            pl.semaphore_wait(barrier, owners - 1 + levels - 1)
            signal(near_sem, partner_of(0), me)
            pl.semaphore_wait(near_sem, 1)
        send_slots(level, level, buffer)
        if level == 0:
            for load in loads[2:] + inv_loads[1:] + cpl_loads[1:]:
                load.wait()
            fold(0)
        else:
            base_ref[level] = settled(level, forward_of(level, residual))
        make_take(level)
        if level + 1 < top:
            make_send(level + 1)
            fold(level + 1)
        arrived = slots_arrived(level)
        incoming = collect(dot(arrived, take_mat[level], TN))
        residual = (b_ref[level + 1].astype(jnp.float32) - incoming).astype(jnp.bfloat16)
        if level + 1 < top:
            blocks = dot(residual, fold_ref[level + 1], NT)

    above = row_mask(top) * settled(top, forward_of(top, residual))
    for level in reversed(range(top)):
        phase = top + level
        above = above.astype(jnp.bfloat16)
        out_ref[level + 1] = above
        send_slots(phase, level, dot(take_mat[level], spread(above.astype(jnp.float32)), NT))
        arrived = slots_arrived(phase)
        rows_in = collect(dot(arrived, send_mat[level], TN)).astype(jnp.bfloat16)
        above = row_mask(level) * (base_ref[level] - dot(rows_in, fold_ref[level]))
    out_ref[0] = above.astype(jnp.bfloat16)

    for phase in range(2 * (levels - 1)):
        for side, count in ((0, owners - 1), (1, owners)):
            pltpu.make_async_copy(
                slot_out.at[phase, side, pl.ds(0, count)],
                slot_in.at[phase, side, pl.ds(0, count)],
                slot_send.at[phase],
            ).wait()


def finish(in_ref, out_ref, sem):
    copy = pltpu.make_async_copy(in_ref, out_ref, sem)
    copy.start()
    copy.wait()


def shards(right_sides, inverses, couplings, widths, targets):
    owners = lax.axis_size("blk")
    right = jnp.swapaxes(right_sides[0, 0], 1, 2)
    inverse, coupling = inverses[0, 0], couplings[0, 0]
    levels, cols, width = right.shape
    rows, pieces = coupling.shape[1], targets.shape[3]
    lanes = rows // pieces * cols
    phases = 2 * (levels - 1)
    slot_rows = 2 * owners * SLOTS
    hbm = pl.BlockSpec(memory_space=pltpu.HBM)
    out = pl.pallas_call(
        functools.partial(kernel, (4, 8, 2)),
        out_shape=jax.ShapeDtypeStruct((levels, cols, width), jnp.bfloat16),
        in_specs=[hbm] * 5,
        out_specs=pl.BlockSpec(memory_space=pltpu.VMEM),
        scratch_shapes=[
            pltpu.SMEM((1, levels), jnp.int32),
            pltpu.VMEM((levels, cols, width), jnp.bfloat16),
            pltpu.VMEM((levels, width, width), jnp.bfloat16),
            pltpu.VMEM((levels - 1, rows, width), jnp.bfloat16),
            pltpu.VMEM((levels - 1, 2, owners, pieces), jnp.int32),
            pltpu.VMEM((levels - 1, slot_rows, rows), jnp.bfloat16),
            pltpu.VMEM((levels - 1, slot_rows, width), jnp.bfloat16),
            pltpu.VMEM((levels - 1, rows, width), jnp.bfloat16),
            pltpu.VMEM((levels - 1, cols, width), jnp.float32),
            pltpu.VMEM((phases, 2, owners, SLOTS, lanes), jnp.bfloat16),
            pltpu.VMEM((phases, 2, owners, SLOTS, lanes), jnp.bfloat16),
            pltpu.SemaphoreType.DMA((4 * levels - 1,)),
            pltpu.SemaphoreType.DMA((phases,)),
            pltpu.SemaphoreType.DMA((phases,)),
            pltpu.SemaphoreType.REGULAR,
        ],
        compiler_params=pltpu.CompilerParams(collective_id=0, has_side_effects=True, vmem_limit_bytes=24 * 2**20),
    )(*[pltpu.with_memory_space_constraint(v, pltpu.HBM) for v in (right, inverse, coupling)], *[pltpu.with_memory_space_constraint(v, pltpu.HBM) for v in (widths[0], targets)])
    out = pl.pallas_call(
        finish,
        out_shape=jax.ShapeDtypeStruct((levels, cols, width), jnp.bfloat16),
        in_specs=[pl.BlockSpec(memory_space=pltpu.VMEM)],
        out_specs=pl.BlockSpec(memory_space=pltpu.HBM),
        scratch_shapes=[pltpu.SemaphoreType.DMA],
        compiler_params=pltpu.CompilerParams(vmem_limit_bytes=4 * 2**20),
    )(out)
    return jnp.swapaxes(out, 1, 2)[None, None]


def solution(mesh):
    return jax.shard_map(
        shards,
        mesh=mesh,
        in_specs=(
            P("leaf", "blk", None, None, None),
            P("leaf", "blk", None, None, None),
            P("leaf", "blk", None, None, None),
            P("leaf", "blk", None),
            P(),
        ),
        out_specs=P("leaf", "blk", None, None, None),
        check_vma=False,
    )
```

```python
import functools

import jax
import jax.numpy as jnp
from jax import lax
from jax.experimental import pallas as pl
from jax.experimental.pallas import tpu as pltpu
from jax.sharding import PartitionSpec as P

BLOCK = 128
SLOTS = 4
MESH = pl.DeviceIdType.MESH
NN = (((1,), (0,)), ((), ()))
NT = (((1,), (1,)), ((), ()))
TN = (((0,), (0,)), ((), ()))


def dot(left, right, dims=NN):
    return lax.dot_general(left, right, dims, preferred_element_type=jnp.float32)


def iota(shape, axis):
    return lax.broadcasted_iota(jnp.int32, shape, axis)


def one_hot(condition):
    return condition.astype(jnp.float32).astype(jnp.bfloat16)


def each_owner(me, sizes, visit):
    xs, zs, cores = sizes
    z, core = lax.rem(lax.div(me, cores), zs), lax.rem(me, cores)
    x = lax.div(me, zs * cores)
    x_order = sorted(range(xs), key=lambda off: -min(off, xs - off))
    columns = [
        lax.rem(x + off, xs) * (zs * cores) + lax.rem(core + 1 + n, cores)
        for off in x_order
        for n in range(cores)
    ]

    def plane(step, carry):
        off = zs // 2 + lax.div(step + 1, 2) * (1 - 2 * lax.rem(step, 2))
        row = lax.rem(z + off, zs) * cores
        for column in columns:
            visit(column + row, False)
        return carry

    lax.fori_loop(0, zs - 1, plane, 0)
    for column in columns[:-1]:
        visit(column + z * cores, False)
    visit(me, True)


def kernel(
    sizes,
    b_hbm,
    inv_hbm,
    cpl_hbm,
    wid_hbm,
    tgt_hbm,
    out_ref,
    wid_ref,
    b_ref,
    inv_ref,
    cpl_ref,
    tbl_ref,
    send_mat,
    take_mat,
    fold_ref,
    base_ref,
    slot_out,
    slot_in,
    load_sem,
    slot_send,
    slot_recv,
    near_sem,
):
    levels, cols, width = b_ref.shape
    rows = cpl_ref.shape[1]
    owners, pieces = tbl_ref.shape[2], tbl_ref.shape[3]
    lanes = rows // pieces * cols
    piece_rows = rows // pieces
    places = width // piece_rows
    leaf_bits = lax.axis_size("leaf").bit_length() - 1
    group, me = lax.axis_index("leaf"), lax.axis_index("blk")
    slot_rows = 2 * owners * SLOTS

    def partner_of(level):
        bit = 1 << level % leaf_bits
        return group + bit - 2 * bit * (group // bit % 2)

    loads = [pltpu.make_async_copy(b_hbm, b_ref, load_sem.at[0])]
    for level in range(levels - 1):
        for side, source in enumerate((group, partner_of(level))):
            loads.append(
                pltpu.make_async_copy(
                    tgt_hbm.at[level, source],
                    tbl_ref.at[level, side],
                    load_sem.at[1 + 2 * level + side],
                )
            )
    base = 2 * levels - 1
    inv_loads = [
        pltpu.make_async_copy(inv_hbm.at[n], inv_ref.at[n], load_sem.at[base + n])
        for n in range(levels)
    ]
    cpl_loads = [
        pltpu.make_async_copy(cpl_hbm.at[n], cpl_ref.at[n], load_sem.at[base + levels + n])
        for n in range(levels - 1)
    ]
    wid_load = pltpu.make_async_copy(wid_hbm, wid_ref, load_sem.at[base + 2 * levels - 1])
    loads[1].start()
    loads[0].start()
    wid_load.start()
    inv_loads[0].start()
    cpl_loads[0].start()
    for copy in loads[2:] + inv_loads[1:] + cpl_loads[1:]:
        copy.start()

    barrier = pltpu.get_barrier_semaphore()

    def signal(semaphore, leaf, blk):
        pl.semaphore_signal(semaphore, inc=1, device_id=(leaf, blk), device_id_type=MESH)

    def greet(owner, last):
        if not last:
            signal(barrier, group, owner)

    for level in range(levels - 1):
        signal(barrier, partner_of(level), me)
    each_owner(me, sizes, greet)

    before = one_hot(iota((pieces, pieces), 0) < iota((pieces, pieces), 1))
    widen = one_hot(iota((pieces, rows), 1) // piece_rows == iota((pieces, rows), 0))
    repeat = one_hot(iota((slot_rows, 2 * owners), 0) // SLOTS == iota((slot_rows, 2 * owners), 1))
    slot_rank = (iota((slot_rows, pieces), 0) % SLOTS).astype(jnp.float32)

    def row_mask(level):
        return (iota((1, width), 1) < wid_ref[0, level] * BLOCK).astype(jnp.float32)

    def make_send(level):
        dest = tbl_ref[level, 0, pl.ds(me, 1), :] // places
        hit = (iota((slot_rows, pieces), 0) // SLOTS == dest).astype(jnp.float32)
        count = dot(hit.astype(jnp.bfloat16), before)
        chosen = jnp.where(count == slot_rank, hit, 0.0).astype(jnp.bfloat16)
        send_mat[level] = dot(chosen, widen).astype(jnp.bfloat16)

    def make_take(level):
        code = jnp.concatenate([tbl_ref[level, 0], tbl_ref[level, 1]], axis=0)
        wanted = iota((2 * owners, 1), 0) // owners * owners + me
        match = (code // places == wanted).astype(jnp.float32)
        spot = dot(repeat, (match * (code % places + 1).astype(jnp.float32)).astype(jnp.bfloat16))
        hit = dot(repeat, match.astype(jnp.bfloat16))
        count = dot(hit.astype(jnp.bfloat16), before)
        spot = jnp.sum(jnp.where(count == slot_rank, spot, 0.0), axis=1, keepdims=True)
        at = (iota((1, width), 1) // piece_rows + 1).astype(jnp.float32)
        take_mat[level] = one_hot(spot == at)

    def spread(value):
        turn = iota(value.shape, 1) % piece_rows
        return jnp.concatenate(
            [jnp.where(turn == i, value, 0.0) for i in range(piece_rows)], axis=0
        ).astype(jnp.bfloat16)

    def collect(value):
        turn = iota((cols, value.shape[1]), 1) % piece_rows
        out = value[:cols]
        for i in range(1, piece_rows):
            out = jnp.where(turn == i, value[i * cols : (i + 1) * cols], out)
        return out

    def send_slots(phase, level, value):
        slot_out[phase] = value.astype(jnp.bfloat16).reshape(2, owners, SLOTS, lanes)
        partner = partner_of(level)

        def send(side, owner, last):
            if side == 0 and last:
                pltpu.make_async_copy(
                    slot_out.at[phase, 0, me], slot_in.at[phase, 0, me], slot_recv.at[phase]
                ).start()
                return
            pltpu.make_async_remote_copy(
                src_ref=slot_out.at[phase, side, owner],
                dst_ref=slot_in.at[phase, side, me],
                send_sem=slot_send.at[phase],
                recv_sem=slot_recv.at[phase],
                device_id=(partner if side else group, owner),
                device_id_type=MESH,
            ).start()

        def send_both(owner, last):
            send(1, owner, last)
            send(0, owner, last)

        if phase == 0:
            pl.semaphore_wait(barrier, owners - 1 + levels - 1)
            signal(near_sem, partner, me)
            each_owner(me, sizes, functools.partial(send, 0))
            pl.semaphore_wait(near_sem, 1)
            each_owner(me, sizes, functools.partial(send, 1))
        else:
            each_owner(me, sizes, send_both)

    def slots_arrived(phase):
        pltpu.make_async_copy(slot_out.at[phase], slot_in.at[phase], slot_recv.at[phase]).wait()
        return slot_in[phase].reshape(slot_rows, lanes)

    def fold(level):
        live = (cpl_ref[level].astype(jnp.float32) * row_mask(level)).astype(jnp.bfloat16)
        fold_ref[level] = dot(live, inv_ref[level]).astype(jnp.bfloat16)

    def forward_of(level, residual):
        return (row_mask(level) * dot(residual, inv_ref[level], NT)).astype(jnp.bfloat16)

    def settled(level, forward):
        return dot(forward, inv_ref[level])

    top = levels - 1
    loads[1].wait()
    make_send(0)
    loads[0].wait()
    inv_loads[0].wait()
    wid_load.wait()
    solved = forward_of(0, b_ref[0])
    cpl_loads[0].wait()
    blocks = dot(solved, cpl_ref[0], NT)
    for level in range(top):
        buffer = jnp.transpose(dot(spread(blocks), send_mat[level], NT))
        send_slots(level, level, buffer)
        if level == 0:
            for load in loads[2:] + inv_loads[1:] + cpl_loads[1:]:
                load.wait()
            fold(0)
            base_ref[0] = settled(0, solved)
        else:
            base_ref[level] = settled(level, forward_of(level, residual))
        make_take(level)
        if level + 1 < top:
            make_send(level + 1)
            fold(level + 1)
        arrived = slots_arrived(level)
        incoming = collect(dot(arrived, take_mat[level], TN))
        residual = (b_ref[level + 1].astype(jnp.float32) - incoming).astype(jnp.bfloat16)
        if level + 1 < top:
            blocks = dot(residual, fold_ref[level + 1], NT)

    above = row_mask(top) * settled(top, forward_of(top, residual))
    for level in reversed(range(top)):
        phase = top + level
        above = above.astype(jnp.bfloat16)
        out_ref[level + 1] = above
        send_slots(phase, level, jnp.transpose(dot(spread(above.astype(jnp.float32)), take_mat[level], NT)))
        arrived = slots_arrived(phase)
        rows_in = collect(dot(arrived, send_mat[level], TN)).astype(jnp.bfloat16)
        above = row_mask(level) * (base_ref[level] - dot(rows_in, fold_ref[level]))
    out_ref[0] = above.astype(jnp.bfloat16)

    for phase in range(2 * (levels - 1)):
        for side, count in ((0, owners - 1), (1, owners)):
            pltpu.make_async_copy(
                slot_out.at[phase, side, pl.ds(0, count)],
                slot_in.at[phase, side, pl.ds(0, count)],
                slot_send.at[phase],
            ).wait()


def finish(in_ref, out_ref, sem):
    copy = pltpu.make_async_copy(in_ref, out_ref, sem)
    copy.start()
    copy.wait()


def shards(right_sides, inverses, couplings, widths, targets):
    owners = lax.axis_size("blk")
    right = jnp.swapaxes(right_sides[0, 0], 1, 2)
    inverse, coupling = inverses[0, 0], couplings[0, 0]
    levels, cols, width = right.shape
    rows, pieces = coupling.shape[1], targets.shape[3]
    lanes = rows // pieces * cols
    phases = 2 * (levels - 1)
    slot_rows = 2 * owners * SLOTS
    hbm = pl.BlockSpec(memory_space=pltpu.HBM)
    out = pl.pallas_call(
        functools.partial(kernel, (4, 8, 2)),
        out_shape=jax.ShapeDtypeStruct((levels, cols, width), jnp.bfloat16),
        in_specs=[hbm] * 5,
        out_specs=pl.BlockSpec(memory_space=pltpu.VMEM),
        scratch_shapes=[
            pltpu.SMEM((1, levels), jnp.int32),
            pltpu.VMEM((levels, cols, width), jnp.bfloat16),
            pltpu.VMEM((levels, width, width), jnp.bfloat16),
            pltpu.VMEM((levels - 1, rows, width), jnp.bfloat16),
            pltpu.VMEM((levels - 1, 2, owners, pieces), jnp.int32),
            pltpu.VMEM((levels - 1, slot_rows, rows), jnp.bfloat16),
            pltpu.VMEM((levels - 1, slot_rows, width), jnp.bfloat16),
            pltpu.VMEM((levels - 1, rows, width), jnp.bfloat16),
            pltpu.VMEM((levels - 1, cols, width), jnp.float32),
            pltpu.VMEM((phases, 2, owners, SLOTS, lanes), jnp.bfloat16),
            pltpu.VMEM((phases, 2, owners, SLOTS, lanes), jnp.bfloat16),
            pltpu.SemaphoreType.DMA((4 * levels - 1,)),
            pltpu.SemaphoreType.DMA((phases,)),
            pltpu.SemaphoreType.DMA((phases,)),
            pltpu.SemaphoreType.REGULAR,
        ],
        compiler_params=pltpu.CompilerParams(collective_id=0, has_side_effects=True, vmem_limit_bytes=24 * 2**20),
    )(*[pltpu.with_memory_space_constraint(v, pltpu.HBM) for v in (right, inverse, coupling)], *[pltpu.with_memory_space_constraint(v, pltpu.HBM) for v in (widths[0], targets)])
    out = pl.pallas_call(
        finish,
        out_shape=jax.ShapeDtypeStruct((levels, cols, width), jnp.bfloat16),
        in_specs=[pl.BlockSpec(memory_space=pltpu.VMEM)],
        out_specs=pl.BlockSpec(memory_space=pltpu.HBM),
        scratch_shapes=[pltpu.SemaphoreType.DMA],
        compiler_params=pltpu.CompilerParams(vmem_limit_bytes=4 * 2**20),
    )(out)
    return jnp.swapaxes(out, 1, 2)[None, None]


def solution(mesh):
    return jax.shard_map(
        shards,
        mesh=mesh,
        in_specs=(
            P("leaf", "blk", None, None, None),
            P("leaf", "blk", None, None, None),
            P("leaf", "blk", None, None, None),
            P("leaf", "blk", None),
            P(),
        ),
        out_specs=P("leaf", "blk", None, None, None),
        check_vma=False,
    )
```

```python
import functools

import jax
import jax.numpy as jnp
from jax import lax
from jax.experimental import pallas as pl
from jax.experimental.pallas import tpu as pltpu
from jax.sharding import PartitionSpec as P

BLOCK = 128
SLOTS = 4
MESH = pl.DeviceIdType.MESH
NN = (((1,), (0,)), ((), ()))
NT = (((1,), (1,)), ((), ()))
TN = (((0,), (0,)), ((), ()))


def dot(left, right, dims=NN):
    return lax.dot_general(left, right, dims, preferred_element_type=jnp.float32)


def iota(shape, axis):
    return lax.broadcasted_iota(jnp.int32, shape, axis)


def one_hot(condition):
    return condition.astype(jnp.float32).astype(jnp.bfloat16)


def each_owner(me, sizes, visit):
    xs, zs, cores = sizes
    z, core = lax.rem(lax.div(me, cores), zs), lax.rem(me, cores)
    x = lax.div(me, zs * cores)
    x_order = sorted(range(xs), key=lambda off: -min(off, xs - off))
    columns = [
        lax.rem(x + off, xs) * (zs * cores) + lax.rem(core + 1 + n, cores)
        for off in x_order
        for n in range(cores)
    ]

    def plane(step, carry):
        off = zs // 2 + lax.div(step + 1, 2) * (1 - 2 * lax.rem(step, 2))
        row = lax.rem(z + off, zs) * cores
        for column in columns:
            visit(column + row, False)
        return carry

    lax.fori_loop(0, zs - 1, plane, 0)
    for column in columns[:-1]:
        visit(column + z * cores, False)
    visit(me, True)


def kernel(
    sizes,
    b_hbm,
    inv_hbm,
    cpl_hbm,
    wid_hbm,
    tgt_hbm,
    out_ref,
    wid_ref,
    b_ref,
    inv_ref,
    cpl_ref,
    tbl_ref,
    send_mat,
    take_mat,
    take_rows,
    fold_ref,
    base_ref,
    slot_out,
    slot_in,
    load_sem,
    slot_send,
    slot_recv,
    near_sem,
):
    levels, cols, width = b_ref.shape
    rows = cpl_ref.shape[1]
    owners, pieces = tbl_ref.shape[2], tbl_ref.shape[3]
    lanes = rows // pieces * cols
    piece_rows = rows // pieces
    places = width // piece_rows
    leaf_bits = lax.axis_size("leaf").bit_length() - 1
    group, me = lax.axis_index("leaf"), lax.axis_index("blk")
    slot_rows = 2 * owners * SLOTS

    def partner_of(level):
        bit = 1 << level % leaf_bits
        return group + bit - 2 * bit * (group // bit % 2)

    loads = [pltpu.make_async_copy(b_hbm, b_ref, load_sem.at[0])]
    for level in range(levels - 1):
        for side, source in enumerate((group, partner_of(level))):
            loads.append(
                pltpu.make_async_copy(
                    tgt_hbm.at[level, source],
                    tbl_ref.at[level, side],
                    load_sem.at[1 + 2 * level + side],
                )
            )
    base = 2 * levels - 1
    inv_loads = [
        pltpu.make_async_copy(inv_hbm.at[n], inv_ref.at[n], load_sem.at[base + n])
        for n in range(levels)
    ]
    cpl_loads = [
        pltpu.make_async_copy(cpl_hbm.at[n], cpl_ref.at[n], load_sem.at[base + levels + n])
        for n in range(levels - 1)
    ]
    wid_load = pltpu.make_async_copy(wid_hbm, wid_ref, load_sem.at[base + 2 * levels - 1])
    loads[1].start()
    loads[0].start()
    wid_load.start()
    inv_loads[0].start()
    cpl_loads[0].start()
    for copy in loads[2:] + inv_loads[1:] + cpl_loads[1:]:
        copy.start()

    barrier = pltpu.get_barrier_semaphore()

    def signal(semaphore, leaf, blk):
        pl.semaphore_signal(semaphore, inc=1, device_id=(leaf, blk), device_id_type=MESH)

    def greet(owner, last):
        if not last:
            signal(barrier, group, owner)

    for level in range(levels - 1):
        signal(barrier, partner_of(level), me)
    each_owner(me, sizes, greet)

    before = one_hot(iota((pieces, pieces), 0) < iota((pieces, pieces), 1))
    widen = one_hot(iota((pieces, rows), 1) // piece_rows == iota((pieces, rows), 0))
    repeat = one_hot(iota((slot_rows, 2 * owners), 0) // SLOTS == iota((slot_rows, 2 * owners), 1))
    slot_rank = (iota((slot_rows, pieces), 0) % SLOTS).astype(jnp.float32)

    def row_mask(level):
        return (iota((1, width), 1) < wid_ref[0, level] * BLOCK).astype(jnp.float32)

    def make_send(level):
        dest = tbl_ref[level, 0, pl.ds(me, 1), :] // places
        hit = (iota((slot_rows, pieces), 0) // SLOTS == dest).astype(jnp.float32)
        count = dot(hit.astype(jnp.bfloat16), before)
        chosen = jnp.where(count == slot_rank, hit, 0.0).astype(jnp.bfloat16)
        send_mat[level] = dot(chosen, widen).astype(jnp.bfloat16)

    def make_take(level):
        code = jnp.concatenate([tbl_ref[level, 0], tbl_ref[level, 1]], axis=0)
        wanted = iota((2 * owners, 1), 0) // owners * owners + me
        match = (code // places == wanted).astype(jnp.float32)
        spot = dot(repeat, (match * (code % places + 1).astype(jnp.float32)).astype(jnp.bfloat16))
        hit = dot(repeat, match.astype(jnp.bfloat16))
        count = dot(hit.astype(jnp.bfloat16), before)
        spot = jnp.sum(jnp.where(count == slot_rank, spot, 0.0), axis=1, keepdims=True)
        at = (iota((1, width), 1) // piece_rows + 1).astype(jnp.float32)
        take_mat[level] = one_hot(spot == at)
        take_rows[level] = jnp.transpose(take_mat[level])

    def spread(value):
        turn = iota(value.shape, 1) % piece_rows
        return jnp.concatenate(
            [jnp.where(turn == i, value, 0.0) for i in range(piece_rows)], axis=0
        ).astype(jnp.bfloat16)

    def collect(value):
        turn = iota((cols, value.shape[1]), 1) % piece_rows
        out = value[:cols]
        for i in range(1, piece_rows):
            out = jnp.where(turn == i, value[i * cols : (i + 1) * cols], out)
        return out

    def send_slots(phase, level, value):
        slot_out[phase] = value.astype(jnp.bfloat16).reshape(2, owners, SLOTS, lanes)
        partner = partner_of(level)

        def send(side, owner, last):
            if side == 0 and last:
                pltpu.make_async_copy(
                    slot_out.at[phase, 0, me], slot_in.at[phase, 0, me], slot_recv.at[phase]
                ).start()
                return
            pltpu.make_async_remote_copy(
                src_ref=slot_out.at[phase, side, owner],
                dst_ref=slot_in.at[phase, side, me],
                send_sem=slot_send.at[phase],
                recv_sem=slot_recv.at[phase],
                device_id=(partner if side else group, owner),
                device_id_type=MESH,
            ).start()

        def send_both(owner, last):
            send(1, owner, last)
            send(0, owner, last)

        if phase == 0:
            pl.semaphore_wait(barrier, owners - 1 + levels - 1)
            signal(near_sem, partner, me)
            each_owner(me, sizes, functools.partial(send, 0))
            pl.semaphore_wait(near_sem, 1)
            each_owner(me, sizes, functools.partial(send, 1))
        else:
            each_owner(me, sizes, send_both)

    def slots_arrived(phase):
        pltpu.make_async_copy(slot_out.at[phase], slot_in.at[phase], slot_recv.at[phase]).wait()
        return slot_in[phase].reshape(slot_rows, lanes)

    def fold(level):
        live = (cpl_ref[level].astype(jnp.float32) * row_mask(level)).astype(jnp.bfloat16)
        fold_ref[level] = dot(live, inv_ref[level]).astype(jnp.bfloat16)

    def forward_of(level, residual):
        return (row_mask(level) * dot(residual, inv_ref[level], NT)).astype(jnp.bfloat16)

    def settled(level, forward):
        return dot(forward, inv_ref[level])

    top = levels - 1
    loads[1].wait()
    make_send(0)
    loads[0].wait()
    inv_loads[0].wait()
    wid_load.wait()
    solved = forward_of(0, b_ref[0])
    cpl_loads[0].wait()
    blocks = dot(solved, cpl_ref[0], NT)
    for level in range(top):
        buffer = jnp.transpose(dot(spread(blocks), send_mat[level], NT))
        send_slots(level, level, buffer)
        if level == 0:
            for load in loads[2:] + inv_loads[1:] + cpl_loads[1:]:
                load.wait()
            fold(0)
            base_ref[0] = settled(0, solved)
        else:
            base_ref[level] = settled(level, forward_of(level, residual))
        make_take(level)
        if level + 1 < top:
            make_send(level + 1)
            fold(level + 1)
        arrived = slots_arrived(level)
        incoming = collect(dot(arrived, take_mat[level], TN))
        residual = (b_ref[level + 1].astype(jnp.float32) - incoming).astype(jnp.bfloat16)
        if level + 1 < top:
            blocks = dot(residual, fold_ref[level + 1], NT)

    above = row_mask(top) * settled(top, forward_of(top, residual))
    for level in reversed(range(top)):
        phase = top + level
        above = above.astype(jnp.bfloat16)
        out_ref[level + 1] = above
        send_slots(phase, level, jnp.transpose(dot(spread(above.astype(jnp.float32)), take_rows[level])))
        arrived = slots_arrived(phase)
        rows_in = collect(dot(arrived, send_mat[level], TN)).astype(jnp.bfloat16)
        above = row_mask(level) * (base_ref[level] - dot(rows_in, fold_ref[level]))
    out_ref[0] = above.astype(jnp.bfloat16)

    for phase in range(2 * (levels - 1)):
        for side, count in ((0, owners - 1), (1, owners)):
            pltpu.make_async_copy(
                slot_out.at[phase, side, pl.ds(0, count)],
                slot_in.at[phase, side, pl.ds(0, count)],
                slot_send.at[phase],
            ).wait()


def finish(in_ref, out_ref, sem):
    copy = pltpu.make_async_copy(in_ref, out_ref, sem)
    copy.start()
    copy.wait()


def shards(right_sides, inverses, couplings, widths, targets):
    owners = lax.axis_size("blk")
    right = jnp.swapaxes(right_sides[0, 0], 1, 2)
    inverse, coupling = inverses[0, 0], couplings[0, 0]
    levels, cols, width = right.shape
    rows, pieces = coupling.shape[1], targets.shape[3]
    lanes = rows // pieces * cols
    phases = 2 * (levels - 1)
    slot_rows = 2 * owners * SLOTS
    hbm = pl.BlockSpec(memory_space=pltpu.HBM)
    out = pl.pallas_call(
        functools.partial(kernel, (4, 8, 2)),
        out_shape=jax.ShapeDtypeStruct((levels, cols, width), jnp.bfloat16),
        in_specs=[hbm] * 5,
        out_specs=pl.BlockSpec(memory_space=pltpu.VMEM),
        scratch_shapes=[
            pltpu.SMEM((1, levels), jnp.int32),
            pltpu.VMEM((levels, cols, width), jnp.bfloat16),
            pltpu.VMEM((levels, width, width), jnp.bfloat16),
            pltpu.VMEM((levels - 1, rows, width), jnp.bfloat16),
            pltpu.VMEM((levels - 1, 2, owners, pieces), jnp.int32),
            pltpu.VMEM((levels - 1, slot_rows, rows), jnp.bfloat16),
            pltpu.VMEM((levels - 1, slot_rows, width), jnp.bfloat16),
            pltpu.VMEM((levels - 1, width, slot_rows), jnp.bfloat16),
            pltpu.VMEM((levels - 1, rows, width), jnp.bfloat16),
            pltpu.VMEM((levels - 1, cols, width), jnp.float32),
            pltpu.VMEM((phases, 2, owners, SLOTS, lanes), jnp.bfloat16),
            pltpu.VMEM((phases, 2, owners, SLOTS, lanes), jnp.bfloat16),
            pltpu.SemaphoreType.DMA((4 * levels - 1,)),
            pltpu.SemaphoreType.DMA((phases,)),
            pltpu.SemaphoreType.DMA((phases,)),
            pltpu.SemaphoreType.REGULAR,
        ],
        compiler_params=pltpu.CompilerParams(collective_id=0, has_side_effects=True, vmem_limit_bytes=24 * 2**20),
    )(*[pltpu.with_memory_space_constraint(v, pltpu.HBM) for v in (right, inverse, coupling)], *[pltpu.with_memory_space_constraint(v, pltpu.HBM) for v in (widths[0], targets)])
    out = pl.pallas_call(
        finish,
        out_shape=jax.ShapeDtypeStruct((levels, cols, width), jnp.bfloat16),
        in_specs=[pl.BlockSpec(memory_space=pltpu.VMEM)],
        out_specs=pl.BlockSpec(memory_space=pltpu.HBM),
        scratch_shapes=[pltpu.SemaphoreType.DMA],
        compiler_params=pltpu.CompilerParams(vmem_limit_bytes=4 * 2**20),
    )(out)
    return jnp.swapaxes(out, 1, 2)[None, None]


def solution(mesh):
    return jax.shard_map(
        shards,
        mesh=mesh,
        in_specs=(
            P("leaf", "blk", None, None, None),
            P("leaf", "blk", None, None, None),
            P("leaf", "blk", None, None, None),
            P("leaf", "blk", None),
            P(),
        ),
        out_specs=P("leaf", "blk", None, None, None),
        check_vma=False,
    )
```

```python
import functools

import jax
import jax.numpy as jnp
from jax import lax
from jax.experimental import pallas as pl
from jax.experimental.pallas import tpu as pltpu
from jax.sharding import PartitionSpec as P

BLOCK = 128
SLOTS = 4
MESH = pl.DeviceIdType.MESH
NN = (((1,), (0,)), ((), ()))
NT = (((1,), (1,)), ((), ()))
TN = (((0,), (0,)), ((), ()))


def dot(left, right, dims=NN):
    return lax.dot_general(left, right, dims, preferred_element_type=jnp.float32)


def iota(shape, axis):
    return lax.broadcasted_iota(jnp.int32, shape, axis)


def one_hot(condition):
    return condition.astype(jnp.float32).astype(jnp.bfloat16)


def each_owner(me, sizes, visit):
    xs, zs, cores = sizes
    z, core = lax.rem(lax.div(me, cores), zs), lax.rem(me, cores)
    x = lax.div(me, zs * cores)
    x_order = sorted(range(xs), key=lambda off: -min(off, xs - off))
    columns = [
        lax.rem(x + off, xs) * (zs * cores) + lax.rem(core + 1 + n, cores)
        for off in x_order
        for n in range(cores)
    ]

    def plane(step, carry):
        off = zs // 2 + lax.div(step + 1, 2) * (1 - 2 * lax.rem(step, 2))
        row = lax.rem(z + off, zs) * cores
        for column in columns:
            visit(column + row, False)
        return carry

    lax.fori_loop(0, zs - 1, plane, 0)
    for column in columns[:-1]:
        visit(column + z * cores, False)
    visit(me, True)


def kernel(
    sizes,
    b_hbm,
    inv_hbm,
    cpl_hbm,
    wid_hbm,
    tgt_hbm,
    out_ref,
    wid_ref,
    b_ref,
    inv_ref,
    cpl_ref,
    tbl_ref,
    send_mat,
    take_mat,
    take_rows,
    fold_ref,
    base_ref,
    slot_out,
    slot_in,
    load_sem,
    slot_send,
    slot_recv,
    near_sem,
):
    levels, cols, width = b_ref.shape
    rows = cpl_ref.shape[1]
    owners, pieces = tbl_ref.shape[2], tbl_ref.shape[3]
    lanes = rows // pieces * cols
    piece_rows = rows // pieces
    places = width // piece_rows
    leaf_bits = lax.axis_size("leaf").bit_length() - 1
    group, me = lax.axis_index("leaf"), lax.axis_index("blk")
    slot_rows = 2 * owners * SLOTS

    def partner_of(level):
        bit = 1 << level % leaf_bits
        return group + bit - 2 * bit * (group // bit % 2)

    loads = [pltpu.make_async_copy(b_hbm, b_ref, load_sem.at[0])]
    for level in range(levels - 1):
        for side, source in enumerate((group, partner_of(level))):
            loads.append(
                pltpu.make_async_copy(
                    tgt_hbm.at[level, source],
                    tbl_ref.at[level, side],
                    load_sem.at[1 + 2 * level + side],
                )
            )
    base = 2 * levels - 1
    inv_loads = [
        pltpu.make_async_copy(inv_hbm.at[part], inv_ref.at[part], load_sem.at[base + n])
        for n, part in enumerate((pl.ds(0, 1), pl.ds(1, levels - 1)))
    ]
    cpl_loads = [
        pltpu.make_async_copy(cpl_hbm.at[part], cpl_ref.at[part], load_sem.at[base + 2 + n])
        for n, part in enumerate((pl.ds(0, 1), pl.ds(1, levels - 2)))
    ]
    wid_load = pltpu.make_async_copy(wid_hbm, wid_ref, load_sem.at[base + 4])
    loads[1].start()
    loads[0].start()
    wid_load.start()
    inv_loads[0].start()
    cpl_loads[0].start()
    for copy in loads[2:] + inv_loads[1:] + cpl_loads[1:]:
        copy.start()

    barrier = pltpu.get_barrier_semaphore()

    def signal(semaphore, leaf, blk):
        pl.semaphore_signal(semaphore, inc=1, device_id=(leaf, blk), device_id_type=MESH)

    def greet(owner, last):
        if not last:
            signal(barrier, group, owner)

    for level in range(levels - 1):
        signal(barrier, partner_of(level), me)
    each_owner(me, sizes, greet)

    before = one_hot(iota((pieces, pieces), 0) < iota((pieces, pieces), 1))
    widen = one_hot(iota((pieces, rows), 1) // piece_rows == iota((pieces, rows), 0))
    repeat = one_hot(iota((slot_rows, 2 * owners), 0) // SLOTS == iota((slot_rows, 2 * owners), 1))
    slot_rank = (iota((slot_rows, pieces), 0) % SLOTS).astype(jnp.float32)

    def row_mask(level):
        return (iota((1, width), 1) < wid_ref[0, level] * BLOCK).astype(jnp.float32)

    def make_send(level):
        dest = tbl_ref[level, 0, pl.ds(me, 1), :] // places
        hit = (iota((slot_rows, pieces), 0) // SLOTS == dest).astype(jnp.float32)
        count = dot(hit.astype(jnp.bfloat16), before)
        chosen = jnp.where(count == slot_rank, hit, 0.0).astype(jnp.bfloat16)
        send_mat[level] = dot(chosen, widen).astype(jnp.bfloat16)

    def make_take(level):
        code = jnp.concatenate([tbl_ref[level, 0], tbl_ref[level, 1]], axis=0)
        wanted = iota((2 * owners, 1), 0) // owners * owners + me
        match = (code // places == wanted).astype(jnp.float32)
        spot = dot(repeat, (match * (code % places + 1).astype(jnp.float32)).astype(jnp.bfloat16))
        hit = dot(repeat, match.astype(jnp.bfloat16))
        count = dot(hit.astype(jnp.bfloat16), before)
        spot = jnp.sum(jnp.where(count == slot_rank, spot, 0.0), axis=1, keepdims=True)
        at = (iota((1, width), 1) // piece_rows + 1).astype(jnp.float32)
        take_mat[level] = one_hot(spot == at)
        take_rows[level] = jnp.transpose(take_mat[level])

    def spread(value):
        turn = iota(value.shape, 1) % piece_rows
        return jnp.concatenate(
            [jnp.where(turn == i, value, 0.0) for i in range(piece_rows)], axis=0
        ).astype(jnp.bfloat16)

    def collect(value):
        turn = iota((cols, value.shape[1]), 1) % piece_rows
        out = value[:cols]
        for i in range(1, piece_rows):
            out = jnp.where(turn == i, value[i * cols : (i + 1) * cols], out)
        return out

    def send_slots(phase, level, value):
        slot_out[phase] = value.astype(jnp.bfloat16).reshape(2, owners, SLOTS, lanes)
        partner = partner_of(level)

        def send(side, owner, last):
            if side == 0 and last:
                pltpu.make_async_copy(
                    slot_out.at[phase, 0, me], slot_in.at[phase, 0, me], slot_recv.at[phase]
                ).start()
                return
            pltpu.make_async_remote_copy(
                src_ref=slot_out.at[phase, side, owner],
                dst_ref=slot_in.at[phase, side, me],
                send_sem=slot_send.at[phase],
                recv_sem=slot_recv.at[phase],
                device_id=(partner if side else group, owner),
                device_id_type=MESH,
            ).start()

        def send_both(owner, last):
            send(1, owner, last)
            send(0, owner, last)

        if phase == 0:
            pl.semaphore_wait(barrier, owners - 1 + levels - 1)
            signal(near_sem, partner, me)
            each_owner(me, sizes, functools.partial(send, 0))
            pl.semaphore_wait(near_sem, 1)
            each_owner(me, sizes, functools.partial(send, 1))
        else:
            each_owner(me, sizes, send_both)

    def slots_arrived(phase):
        pltpu.make_async_copy(slot_out.at[phase], slot_in.at[phase], slot_recv.at[phase]).wait()
        return slot_in[phase].reshape(slot_rows, lanes)

    def fold(level):
        live = (cpl_ref[level].astype(jnp.float32) * row_mask(level)).astype(jnp.bfloat16)
        fold_ref[level] = dot(live, inv_ref[level]).astype(jnp.bfloat16)

    def forward_of(level, residual):
        return (row_mask(level) * dot(residual, inv_ref[level], NT)).astype(jnp.bfloat16)

    def settled(level, forward):
        return dot(forward, inv_ref[level])

    top = levels - 1
    loads[1].wait()
    make_send(0)
    loads[0].wait()
    inv_loads[0].wait()
    wid_load.wait()
    solved = forward_of(0, b_ref[0])
    cpl_loads[0].wait()
    blocks = dot(solved, cpl_ref[0], NT)
    for level in range(top):
        buffer = jnp.transpose(dot(spread(blocks), send_mat[level], NT))
        send_slots(level, level, buffer)
        if level == 0:
            for load in loads[2:] + inv_loads[1:] + cpl_loads[1:]:
                load.wait()
            fold(0)
            base_ref[0] = settled(0, solved)
        else:
            base_ref[level] = settled(level, forward_of(level, residual))
        make_take(level)
        if level + 1 < top:
            make_send(level + 1)
            fold(level + 1)
        arrived = slots_arrived(level)
        incoming = collect(dot(arrived, take_mat[level], TN))
        residual = (b_ref[level + 1].astype(jnp.float32) - incoming).astype(jnp.bfloat16)
        if level + 1 < top:
            blocks = dot(residual, fold_ref[level + 1], NT)

    above = row_mask(top) * settled(top, forward_of(top, residual))
    for level in reversed(range(top)):
        phase = top + level
        above = above.astype(jnp.bfloat16)
        out_ref[level + 1] = above
        send_slots(phase, level, jnp.transpose(dot(spread(above.astype(jnp.float32)), take_rows[level])))
        arrived = slots_arrived(phase)
        rows_in = collect(dot(arrived, send_mat[level], TN)).astype(jnp.bfloat16)
        above = row_mask(level) * (base_ref[level] - dot(rows_in, fold_ref[level]))
    out_ref[0] = above.astype(jnp.bfloat16)

    for phase in range(2 * (levels - 1)):
        for side, count in ((0, owners - 1), (1, owners)):
            pltpu.make_async_copy(
                slot_out.at[phase, side, pl.ds(0, count)],
                slot_in.at[phase, side, pl.ds(0, count)],
                slot_send.at[phase],
            ).wait()


def finish(in_ref, out_ref, sem):
    copy = pltpu.make_async_copy(in_ref, out_ref, sem)
    copy.start()
    copy.wait()


def shards(right_sides, inverses, couplings, widths, targets):
    owners = lax.axis_size("blk")
    right = jnp.swapaxes(right_sides[0, 0], 1, 2)
    inverse, coupling = inverses[0, 0], couplings[0, 0]
    levels, cols, width = right.shape
    rows, pieces = coupling.shape[1], targets.shape[3]
    lanes = rows // pieces * cols
    phases = 2 * (levels - 1)
    slot_rows = 2 * owners * SLOTS
    hbm = pl.BlockSpec(memory_space=pltpu.HBM)
    out = pl.pallas_call(
        functools.partial(kernel, (4, 8, 2)),
        out_shape=jax.ShapeDtypeStruct((levels, cols, width), jnp.bfloat16),
        in_specs=[hbm] * 5,
        out_specs=pl.BlockSpec(memory_space=pltpu.VMEM),
        scratch_shapes=[
            pltpu.SMEM((1, levels), jnp.int32),
            pltpu.VMEM((levels, cols, width), jnp.bfloat16),
            pltpu.VMEM((levels, width, width), jnp.bfloat16),
            pltpu.VMEM((levels - 1, rows, width), jnp.bfloat16),
            pltpu.VMEM((levels - 1, 2, owners, pieces), jnp.int32),
            pltpu.VMEM((levels - 1, slot_rows, rows), jnp.bfloat16),
            pltpu.VMEM((levels - 1, slot_rows, width), jnp.bfloat16),
            pltpu.VMEM((levels - 1, width, slot_rows), jnp.bfloat16),
            pltpu.VMEM((levels - 1, rows, width), jnp.bfloat16),
            pltpu.VMEM((levels - 1, cols, width), jnp.float32),
            pltpu.VMEM((phases, 2, owners, SLOTS, lanes), jnp.bfloat16),
            pltpu.VMEM((phases, 2, owners, SLOTS, lanes), jnp.bfloat16),
            pltpu.SemaphoreType.DMA((2 * levels + 4,)),
            pltpu.SemaphoreType.DMA((phases,)),
            pltpu.SemaphoreType.DMA((phases,)),
            pltpu.SemaphoreType.REGULAR,
        ],
        compiler_params=pltpu.CompilerParams(collective_id=0, has_side_effects=True, vmem_limit_bytes=24 * 2**20),
    )(*[pltpu.with_memory_space_constraint(v, pltpu.HBM) for v in (right, inverse, coupling)], *[pltpu.with_memory_space_constraint(v, pltpu.HBM) for v in (widths[0], targets)])
    out = pl.pallas_call(
        finish,
        out_shape=jax.ShapeDtypeStruct((levels, cols, width), jnp.bfloat16),
        in_specs=[pl.BlockSpec(memory_space=pltpu.VMEM)],
        out_specs=pl.BlockSpec(memory_space=pltpu.HBM),
        scratch_shapes=[pltpu.SemaphoreType.DMA],
        compiler_params=pltpu.CompilerParams(vmem_limit_bytes=4 * 2**20),
    )(out)
    return jnp.swapaxes(out, 1, 2)[None, None]


def solution(mesh):
    return jax.shard_map(
        shards,
        mesh=mesh,
        in_specs=(
            P("leaf", "blk", None, None, None),
            P("leaf", "blk", None, None, None),
            P("leaf", "blk", None, None, None),
            P("leaf", "blk", None),
            P(),
        ),
        out_specs=P("leaf", "blk", None, None, None),
        check_vma=False,
    )
```
